256 devices in a mesh: space: 8 (over y, core), dev: 32 (over x, z).
Axes of the slice: x: 4, y: 4, z: 8, core: 2. Of those that a mesh axis runs over, the one named last changes fastest.
Arguments:
- density_matrix: float32 [4096, 4096], P(('space', 'dev')), may hold values from -0.2 to 0.2
- basis: float32 [512, 384, 1024], P(('space', 'dev')), may hold values from -1.6 to 1.6
- union: int32 [512, 8], P(('space', 'dev')), may hold values from 0 to 31, as said below
- weights: float32 [512, 384], P(('space', 'dev')), may hold values from 0.2 to 2
- in_scale: float32 [256], replicated, may hold values from 0.3 to 3
- in_shift: float32 [256], replicated, may hold values from -1 to 1
- hidden_weight: float32 [256, 256], replicated, may hold values from -0.375 to 0.375
- hidden_bias: float32 [256], replicated, may hold values from -3 to 3
- out_weight: float32 [256], replicated, may hold values from -0.375 to 0.375
Outputs:
- density: float32 [512, 384], P(('space', 'dev'))
- potential: float32 [4096, 4096], P(('space', 'dev'))
The draws below stay inside these ranges and needn't reach their ends.
Inputs may be any that keep to these rules, and one draw needn't show every extreme that they name: `union`: row b lists 8 distinct tiles, all among tiles (g - 1) * 4 to (g + 2) * 4 - 1, where g = b // 64.
All inputs are finite; a program needn't handle non-finite values.
Results may differ from the reference program's by a relative error of at most 0.00011.
Values sent between devices are 32-bit elements; how exact they have to be, the bound alone decides.
A program may use at most 128 MiB of HBM per device.

```python
import math
import jax
import jax.numpy as jnp
from jax import lax

ORB = 4096
TILE = 128
U = 8
NET_WIDTH = 256
PB = 384
NTB = 32
REGION = 4
GROUP_BATCHES = 64
BATCHES = 512


def draw_union(key, part):
    batch_keys = jax.random.split(key, BATCHES)
    groups = jnp.arange(BATCHES, dtype=jnp.int32) // GROUP_BATCHES

    def pick_tiles(batch_key, group_of):
        shuffled = jax.random.permutation(batch_key, 3 * REGION).astype(jnp.int32)
        candidate = (group_of - 1) * REGION + shuffled
        usable = (candidate >= 0) & (candidate < NTB)
        position = jnp.arange(3 * REGION, dtype=jnp.int32)
        scores = jnp.where(usable, position, position + 4 * REGION)
        ranking = jnp.argsort(scores, stable=True)
        return candidate[ranking[:U]]
    return jax.vmap(pick_tiles)(batch_keys, groups).astype(jnp.int32)


def shard_levels(stream_key, dims, pieces, low, top_value):
    gain = 1.0
    for axis_at, shards_of in pieces:
        heights = jax.random.uniform(jax.random.fold_in(jax.random.fold_in(stream_key, 6), axis_at), (shards_of,), jnp.float32, low / len(pieces), top_value / len(pieces))
        gain = gain * jnp.repeat(jnp.exp(heights), dims[axis_at] // shards_of).reshape((-1,) + (1,) * (len(dims) - 1 - axis_at))
    return gain


def centred(key, dims, width, reach, cuts=(), kind=jnp.bfloat16):
    drawn = jax.random.normal(key, dims, jnp.float32) * width
    if len(cuts) > 0:
        drawn = shard_levels(key, dims, cuts, -0.22, 0.18) * drawn
    return jnp.clip(drawn, min=-reach, max=reach).astype(kind)


def setup_inputs(seed: int = 0) -> dict:
    streams_of = jax.random.split(jax.random.key(seed), 10)
    return {
        "density_matrix": centred(streams_of[0], (ORB, ORB), 0.025, 0.2, ((0, 256),), jnp.float32),
        "basis": centred(streams_of[1], (BATCHES, PB, U * TILE), 0.2, 1.6, ((0, 256),), jnp.float32),
        "union": draw_union(jax.random.fold_in(streams_of[9], 71), 0),
        "weights": jnp.clip(jnp.exp(math.log(2.0) - 2.3025851 * jax.random.uniform(streams_of[3], (BATCHES, PB), jnp.float32) ** shard_levels(streams_of[3], (BATCHES, PB), ((0, 256),), -0.2, 0.2)), 0.2, 2.0),
        "in_scale": jnp.clip(jnp.exp(jax.random.uniform(streams_of[4], (NET_WIDTH,), jnp.float32, math.log(0.3), math.log(3.0))), 0.3, 3.0),
        "in_shift": jnp.clip(jax.random.uniform(streams_of[5], (NET_WIDTH,), jnp.float32, -1.0, 1.0), -1.0, 1.0),
        "hidden_weight": centred(streams_of[6], (NET_WIDTH, NET_WIDTH), NET_WIDTH ** -0.5, 0.375, (), jnp.float32),
        "hidden_bias": centred(streams_of[7], (NET_WIDTH,), 0.5, 3.0, (), jnp.float32),
        "out_weight": centred(streams_of[8], (NET_WIDTH,), NET_WIDTH ** -0.5, 0.375, (), jnp.float32),
    }


highest = lax.Precision.HIGHEST


def potential_net(point_rho, in_scale, in_shift, hidden_weight, hidden_bias, out_weight):
    first_layer = jnp.tanh(point_rho[:, None] * in_scale[None, :] + in_shift[None, :])
    pre_act = jnp.dot(first_layer, hidden_weight, precision=highest, preferred_element_type=jnp.float32) + hidden_bias[None, :]
    second = jax.nn.silu(pre_act)
    return jnp.dot(second, out_weight, precision=highest, preferred_element_type=jnp.float32)


def reference(density_matrix, basis, union, weights, in_scale, in_shift, hidden_weight, hidden_bias, out_weight):
    tile_count = ORB // TILE
    union_width = U * TILE
    blocks = density_matrix.reshape(tile_count, TILE, tile_count, TILE)

    def add_batch(accumulated, batch_data):
        values, chosen, quad_weights = batch_data
        sub_block = blocks[chosen[:, None], :, chosen[None, :], :]
        sub_block = sub_block.transpose(0, 2, 1, 3).reshape(union_width, union_width)
        projected = jnp.dot(values, sub_block, precision=highest, preferred_element_type=jnp.float32)
        point_rho = jnp.sum(projected * values, axis=1)
        point_pot = potential_net(point_rho, in_scale, in_shift, hidden_weight, hidden_bias, out_weight)
        scaled = values * (quad_weights * point_pot)[:, None]
        product = lax.dot_general(scaled, values, (((0,), (0,)), ((), ())), precision=highest, preferred_element_type=jnp.float32)
        term_tile = product.reshape(U, TILE, U, TILE).transpose(0, 2, 1, 3)
        accumulated = accumulated.at[chosen[:, None], :, chosen[None, :], :].add(term_tile)
        return accumulated, point_rho

    initial = jnp.zeros((tile_count, TILE, tile_count, TILE), jnp.float32)
    accumulated, density = lax.scan(add_batch, initial, (basis, union, weights))
    return density, accumulated.reshape(ORB, ORB)
```

```python
import functools
import heapq

import jax
import jax.numpy as jnp
from jax import lax
from jax.experimental import pallas as pl
from jax.experimental.pallas import tpu as pltpu
from jax.sharding import PartitionSpec as P

MESH = pl.DeviceIdType.MESH
TILE = 128
U = 8
NX, NZ = 4, 8
NS = 8
ROWS = 16
WT = 12
ND = 7
STRIPS = 3 * ND
PB = 384
NP = 2 * PB
NPAIR = WT // 2
SPAN = 8 * TILE
WIDE = (WT + 6) * TILE
GRID_TILES = 32

CLASSES = (
    (0, 6, True, 1),
    (6, 12, True, -1),
    (12, 17, False, 1),
    (17, 21, False, -1),
)


def class_nodes(sign):
    xs = (0, 1, -1, 2 * sign)
    zs = (0, 1, -1, 2, -2, 3, -3, 4 * sign)
    return [(dx, dz) for dx in xs for dz in zs if (dx, dz) != (0, 0)]


def parent_of(node, z_first):
    dx, dz = node
    step_x = (dx > 0) - (dx < 0)
    step_z = (dz > 0) - (dz < 0)
    if z_first:
        return ((dx - step_x, dz), (step_x, 0)) if dx else ((0, dz - step_z), (0, step_z))
    return ((dx, dz - step_z), (0, step_z)) if dz else ((dx - step_x, 0), (step_x, 0))


def plan():
    children = {}
    for c, (lo, hi, z_first, sign) in enumerate(CLASSES):
        for node in class_nodes(sign):
            par, step = parent_of(node, z_first)
            children.setdefault((c, par), []).append((c, node, step))
    latency = 14.0
    free = {}
    heap = []
    order = []

    def push(now, kids):
        for c, node, step in kids:
            lo, hi = CLASSES[c][:2]
            start = max(now, free.get(step, 0.0))
            free[step] = start + (hi - lo)
            heapq.heappush(heap, (free[step] + latency, c, node, step))

    first, later = [], []
    for c, (lo, hi, z_first, sign) in enumerate(CLASSES):
        for kid in children[(c, (0, 0))]:
            lead = (kid[2][1] != 0) == z_first
            (first if lead else later).append(kid)
    roots = first + later
    push(0.0, roots)
    while heap:
        now, c, node, step = heapq.heappop(heap)
        order.append((c, node, step))
        push(now, children.get((c, node), []))
    return roots, order, children


ROOTS, ORDER, CHILDREN = plan()
NODE_ID = {}
for _c in range(len(CLASSES)):
    for _k, _node in enumerate(class_nodes(CLASSES[_c][3])):
        NODE_ID[(_c, _node)] = _k
NN = NX * NZ - 1


def split(value):
    high = value.astype(jnp.bfloat16)
    low = (value - high.astype(jnp.float32)).astype(jnp.bfloat16)
    return high, low


def swap_groups(parts):
    lane = lax.broadcasted_iota(jnp.int32, (ROWS, TILE), 1) // ROWS
    parts = list(parts)
    for bit in range(3):
        d = 1 << bit
        upper = (lane // d) % 2 == 1
        for i in range(8):
            if i & d:
                continue
            a, b = parts[i], parts[i + d]
            parts[i] = jnp.where(upper, pltpu.roll(b, ROWS * d, 1), a)
            parts[i + d] = jnp.where(upper, b, pltpu.roll(a, TILE - ROWS * d, 1))
    return parts


def fdot(a, b):
    return jnp.dot(a, b, preferred_element_type=jnp.float32)


def kernel(
    union_ref, rows_ref, basis_hbm, weights_ref, scale_ref, shift_ref, hidden_ref, bias_ref, out_w_ref,
    density_ref, potential_ref,
    basis_ref, full_ref, v3_ref, bth_ref, btl_ref, sh_ref, sl_ref, t3_ref,
    gath_ref, part_ref, land_ref,
    mine_ref, msend_ref, mrecv_ref, tt_ref, dsend_ref, dland_ref, tland_ref,
    mrecv2_ref, msend2_ref, ss_ref, dland2_ref, tland2_ref,
    basis_sem, ag_send, ag_recv, rs_send, rs_recv,
    m_send, m_recv, d_send, d_recv, t_send, t_recv,
    m2_send, m2_recv, d2_send, d2_recv, t2_send, t2_recv,
):
    region = lax.axis_index("space")
    dev = lax.axis_index("dev")
    x = dev // NZ
    z = dev % NZ

    def device(dr, dx, dz):
        return {
            "space": (region + dr + NS) % NS,
            "dev": ((x + dx + 2 * NX) % NX) * NZ + (z + dz + NZ) % NZ,
        }

    load = pltpu.make_async_copy(basis_hbm, basis_ref, basis_sem)
    load.start()

    barrier = pltpu.get_barrier_semaphore()
    peers = [(0, 0, dz) for dz in range(1, NZ)]
    peers += [(dr, dx, 0) for dr in (-1, 0, 1) for dx in range(NX) if (dr, dx) != (0, 0)]
    for peer in peers:
        pl.semaphore_signal(barrier, inc=1, device_id=device(*peer), device_id_type=MESH)

    sent = []

    def remote(src, dst, send_sem, recv_sem, where):
        return pltpu.make_async_remote_copy(
            src_ref=src, dst_ref=dst, send_sem=send_sem, recv_sem=recv_sem,
            device_id=device(*where), device_id_type=MESH,
        )

    def go(*args):
        copy = remote(*args)
        copy.start()
        sent.append(copy)

    def row_tile(tile):
        tile = (tile + 2 * GRID_TILES) % GRID_TILES
        return pl.ds(pl.multiple_of(tile * TILE, TILE), TILE)

    my_tile = region * 4 + x

    for dr in (-1, 0, 1):
        i = x + 4 * (1 - dr)
        base = 4 * (region + dr - 1)
        for delta in range(ND):
            strip = rows_ref[:, row_tile(base + (i + delta) % WT)]
            if dr == 0:
                mine_ref[ND + delta] = strip
            else:
                dsend_ref[(dr + 1) // 2, delta] = strip
    slots = []
    for delta in range(1, 6):
        for wrap in range(2):
            slots.append(rows_ref[:, row_tile(my_tile - delta + WT * wrap)])
    zero = jnp.zeros((ROWS, TILE), jnp.float32)
    slots += [zero] * (16 - len(slots))
    for grp in range(2):
        for zz, part in enumerate(swap_groups(slots[8 * grp : 8 * grp + 8])):
            msend_ref[zz, grp] = part

    pl.semaphore_wait(barrier, len(peers))
    for k in range(1, NZ):
        go(msend_ref.at[(z + k) % NZ], mrecv_ref.at[z], m_send.at[k - 1], m_recv.at[k - 1], (0, 0, k))
    for k, dr in enumerate((-1, 1)):
        go(dsend_ref.at[k], dland_ref.at[k], d_send.at[k], d_recv.at[k], (dr, 0, 0))
    mrecv_ref[z] = msend_ref[z]

    for k in range(1, NZ):
        slot = mrecv_ref.at[(z - k + NZ) % NZ]
        remote(slot, slot, m_send.at[k - 1], m_recv.at[k - 1], (0, 0, k)).wait_recv()
    for grp in range(2):
        stacked = mrecv_ref[:, grp].reshape(TILE, TILE).T
        for e in range(8):
            if 8 * grp + e < 10:
                tt_ref[8 * grp + e] = stacked[ROWS * e : ROWS * (e + 1)]

    kinds = [(k, dr, delta) for k, (dr, delta) in enumerate((r, d) for r in (-1, 0, 1) for d in range(1, 6))]
    for k, dr, delta in kinds:
        j = x + 4 * (1 - dr)
        wrap = 1 - (j - delta + WT) // WT
        e = 2 * (delta - 1) + wrap
        if dr == 0 and delta == 4:
            tland_ref[k] = tt_ref[e]
        else:
            go(tt_ref.at[e], tland_ref.at[k], t_send.at[k], t_recv.at[k], (dr, -delta, 0))

    for k, dr in enumerate((-1, 1)):
        slot = dland_ref.at[k]
        remote(slot, slot, d_send.at[k], d_recv.at[k], (dr, 0, 0)).wait_recv()
        first = ND * (1 - dr)
        mine_ref[pl.ds(first, ND)] = dland_ref[k]
    for k, dr, delta in kinds:
        if not (dr == 0 and delta == 4):
            slot = tland_ref.at[k]
            remote(slot, slot, t_send.at[k], t_recv.at[k], (dr, -delta, 0)).wait_recv()
        j = (x + delta) % NX + 4 * (1 - dr)
        i = (j - delta + WT) % WT
        s = (i // 4) * ND + delta
        mine_ref[s] += tland_ref[k]
    gath_ref[x, z] = mine_ref[...]

    def block(ref, dx, dz, lo, hi):
        return ref.at[(x - dx + 2 * NX) % NX, (z - dz + NZ) % NZ, lo:hi]

    def forward(c, node, step, at):
        lo, hi = CLASSES[c][:2]
        k = c * NN + NODE_ID[(c, node)]
        view = block(gath_ref, at[0], at[1], lo, hi)
        go(view, view, ag_send.at[k], ag_recv.at[k], (0, step[0], step[1]))

    for c, node, step in ROOTS:
        forward(c, node, step, (0, 0))

    first_tile = 4 * (region - 1)

    def prepare(t, carry):
        for b in range(2):
            value = None
            for s in range(U):
                hit = (union_ref[b, s] == first_tile + t).astype(jnp.float32)
                term = basis_ref[b, :, s * TILE : (s + 1) * TILE] * hit
                value = term if value is None else value + term
            high, low = split(value)
            rows = pl.ds(b * PB, PB)
            full_ref[rows, pl.ds(pl.multiple_of(t * TILE, TILE), TILE)] = value

            @pl.when(t < 6)
            def _():
                full_ref[rows, pl.ds(pl.multiple_of((t + WT) * TILE, TILE), TILE)] = value

            p = t // 2
            off = (t % 2) * TILE
            for part, src in enumerate((high, low, high)):
                v3_ref[p, rows, pl.ds(pl.multiple_of(off + 256 * part, TILE), TILE)] = src
            high_t, low_t = split(value.T)
            tile_rows = pl.ds(pl.multiple_of(t * TILE, TILE), TILE)
            bth_ref[tile_rows, b * PB : (b + 1) * PB] = high_t
            btl_ref[tile_rows, b * PB : (b + 1) * PB] = low_t
        return carry

    t3_ref[...] = jnp.zeros_like(t3_ref)
    pieces = {6: (0, 2), 18: (2, 4), 30: (4, 6), 42: (6, 8), 54: (8, 10), 66: (10, 12)}
    load.wait()
    for n, (c, node, step) in enumerate(ORDER):
        lo, hi = CLASSES[c][:2]
        k = c * NN + NODE_ID[(c, node)]
        view = block(gath_ref, node[0], node[1], lo, hi)
        remote(view, view, ag_send.at[k], ag_recv.at[k], (0, step[0], step[1])).wait_recv()
        for kid in CHILDREN.get((c, node), []):
            forward(*kid, node)
        if n in pieces:
            lax.fori_loop(*pieces[n], prepare, 0)

    def pair_density(p, acc):
        for h in range(2):
            i = 2 * p + h
            for delta in range(ND):
                tile = gath_ref[i % 4, :, (i // 4) * ND + delta].reshape(TILE, TILE)
                high, low = split(tile)
                cols = slice((h + delta) * TILE, (h + delta + 1) * TILE)
                t3_ref[TILE * h : TILE * (h + 1), cols] = high
                t3_ref[256 + TILE * h : 256 + TILE * (h + 1), cols] = high
                t3_ref[512 + TILE * h : 512 + TILE * (h + 1), cols] = low
        for q in range(4):
            res = fdot(v3_ref[p], t3_ref[:, 256 * q : 256 * (q + 1)])
            other = full_ref[:, pl.ds(pl.multiple_of(p * 256 + 256 * q, TILE), 256)]
            res = res * other
            acc = acc + res[:, :TILE] + res[:, TILE:]
        return acc

    acc = lax.fori_loop(0, NPAIR, pair_density, jnp.zeros((NP, TILE), jnp.float32))
    rho = jnp.sum(acc, axis=1, keepdims=True)

    hid_high, hid_low = split(hidden_ref[...])
    first = jnp.tanh(rho * scale_ref[...] + shift_ref[...])
    high, low = split(first)
    pre = fdot(high, hid_high) + fdot(low, hid_high) + fdot(high, hid_low) + bias_ref[...]
    second = pre / (1.0 + jnp.exp(-pre))
    pot = jnp.sum(second * out_w_ref[...], axis=1, keepdims=True)
    for b in range(2):
        rho_b = jnp.broadcast_to(rho[b * PB : (b + 1) * PB], (PB, TILE)).T
        density_ref[b : b + 1, :] = rho_b[0:1]
        w_b = jnp.broadcast_to(weights_ref[b : b + 1, :], (TILE, PB)).T
        factor = w_b[:, 0:1] * pot[b * PB : (b + 1) * PB]

        def scale_tile(t, carry):
            cols = pl.ds(pl.multiple_of(t * TILE, TILE), TILE)
            rows = pl.ds(b * PB, PB)
            high, low = split(full_ref[rows, cols] * factor)
            sh_ref[rows, cols] = high
            sl_ref[rows, cols] = low
            return carry

        lax.fori_loop(0, WIDE // TILE, scale_tile, 0)

    def pair_part(p, carry):
        rows = pl.ds(pl.multiple_of(p * 256, 256), 256)
        left_high, left_low = bth_ref[rows], btl_ref[rows]
        for q in range(4):
            cols = pl.ds(pl.multiple_of(p * 256 + 256 * q, TILE), 256)
            right_high = sh_ref[:, cols]
            res = fdot(left_high, right_high) + fdot(left_low, right_high) + fdot(left_high, sl_ref[:, cols])
            for h in range(2):
                i = 2 * p + h
                for w in range(2):
                    delta = 2 * q + w - h
                    if 0 <= delta < ND:
                        piece = res[h * TILE : (h + 1) * TILE, w * TILE : (w + 1) * TILE]
                        part_ref[i % 4, :, (i // 4) * ND + delta] = piece.reshape(NZ, ROWS, TILE)
        return carry

    lax.fori_loop(0, NPAIR, pair_part, 0)

    def add_children(c, node):
        lo, hi = CLASSES[c][:2]
        bx, bz = (x - node[0] + 2 * NX) % NX, (z - node[1] + NZ) % NZ
        for _, kid, step in CHILDREN.get((c, node), []):
            k = NODE_ID[(c, kid)]
            slot = land_ref.at[k, lo:hi]
            sem = c * NN + k
            remote(slot, slot, rs_send.at[sem], rs_recv.at[sem], (0, -step[0], -step[1])).wait_recv()
            part_ref[bx, bz, lo:hi] += land_ref[k, lo:hi]

    for c, node, step in reversed(ORDER):
        add_children(c, node)
        lo, hi = CLASSES[c][:2]
        k = NODE_ID[(c, node)]
        go(
            block(part_ref, node[0], node[1], lo, hi), land_ref.at[k, lo:hi],
            rs_send.at[c * NN + k], rs_recv.at[c * NN + k], (0, -step[0], -step[1]),
        )
    for c in reversed(range(len(CLASSES))):
        add_children(c, (0, 0))

    own = part_ref.at[x, z]
    for k, dr in enumerate((-1, 1)):
        go(own.at[pl.ds(ND * (1 + dr), ND)], dland2_ref.at[k], d2_send.at[k], d2_recv.at[k], (dr, 0, 0))
    ss_ref[...] = jnp.zeros_like(ss_ref)

    def transposed_slot(xx, dr, delta):
        j = xx + 4 * (1 - dr)
        wrap = 1 - (j - delta + WT) // WT
        return 2 * (delta - 1) + wrap

    for k, dr, delta in kinds:
        j = (x + delta) % NX + 4 * (1 - dr)
        i = (j - delta + WT) % WT
        s = (i // 4) * ND + delta
        if dr == 0 and delta == 4:
            ss_ref[transposed_slot(x, dr, delta)] += part_ref[x, z, s]
        else:
            go(own.at[s], tland2_ref.at[k], t2_send.at[k], t2_recv.at[k], (-dr, delta, 0))
    for k, dr, delta in kinds:
        if dr == 0 and delta == 4:
            continue
        slot = tland2_ref.at[k]
        remote(slot, slot, t2_send.at[k], t2_recv.at[k], (-dr, delta, 0)).wait_recv()
        ss_ref[transposed_slot(x, dr, delta)] += tland2_ref[k]
    for grp in range(2):
        stacked = ss_ref[8 * grp : 8 * grp + 8].reshape(TILE, TILE).T
        for zz in range(NZ):
            msend2_ref[zz, grp] = stacked[ROWS * zz : ROWS * (zz + 1)]
    for k in range(1, NZ):
        go(msend2_ref.at[(z + k) % NZ], mrecv2_ref.at[z], m2_send.at[k - 1], m2_recv.at[k - 1], (0, 0, k))
    mrecv2_ref[z] = msend2_ref[z]

    potential_ref[...] = jnp.zeros_like(potential_ref)
    for k, dr in enumerate((-1, 1)):
        slot = dland2_ref.at[k]
        remote(slot, slot, d2_send.at[k], d2_recv.at[k], (dr, 0, 0)).wait_recv()
    for dr in (-1, 0, 1):
        i = x + 4 * (1 - dr)
        base = 4 * (region + dr - 1)
        for delta in range(ND):
            cols = row_tile(base + (i + delta) % WT)
            if dr == 0:
                strip = part_ref[x, z, ND + delta]
            else:
                strip = dland2_ref[(1 - dr) // 2, delta]
            potential_ref[:, cols] += strip
    for k in range(1, NZ):
        slot = mrecv2_ref.at[(z - k + NZ) % NZ]
        remote(slot, slot, m2_send.at[k - 1], m2_recv.at[k - 1], (0, 0, k)).wait_recv()
    back = []
    for grp in range(2):
        back += swap_groups([mrecv2_ref[zz, grp] for zz in range(NZ)])
    for delta in range(1, 6):
        for wrap in range(2):
            cols = row_tile(my_tile - delta + WT * wrap)
            potential_ref[:, cols] += back[2 * (delta - 1) + wrap]

    for copy in sent:
        copy.wait_send()


def on_device(density_matrix, basis, union, weights, in_scale, in_shift, hidden_weight, hidden_bias, out_weight):
    vmem = pl.BlockSpec(memory_space=pltpu.VMEM)
    f32, bf16 = jnp.float32, jnp.bfloat16
    dma = pltpu.SemaphoreType.DMA
    count = len(CLASSES) * NN
    scratch = [
        pltpu.VMEM((2, PB, U * TILE), f32),
        pltpu.VMEM((NP, WIDE), f32),
        pltpu.VMEM((NPAIR, NP, 768), bf16),
        pltpu.VMEM((WT * TILE, NP), bf16),
        pltpu.VMEM((WT * TILE, NP), bf16),
        pltpu.VMEM((NP, WIDE), bf16),
        pltpu.VMEM((NP, WIDE), bf16),
        pltpu.VMEM((768, SPAN), bf16),
        pltpu.VMEM((NX, NZ, STRIPS, ROWS, TILE), f32),
        pltpu.VMEM((NX, NZ, STRIPS, ROWS, TILE), f32),
        pltpu.VMEM((NN, STRIPS, ROWS, TILE), f32),
        pltpu.VMEM((STRIPS, ROWS, TILE), f32),
        pltpu.VMEM((NZ, 2, ROWS, TILE), f32),
        pltpu.VMEM((NZ, 2, ROWS, TILE), f32),
        pltpu.VMEM((10, ROWS, TILE), f32),
        pltpu.VMEM((2, ND, ROWS, TILE), f32),
        pltpu.VMEM((2, ND, ROWS, TILE), f32),
        pltpu.VMEM((15, ROWS, TILE), f32),
        pltpu.VMEM((NZ, 2, ROWS, TILE), f32),
        pltpu.VMEM((NZ, 2, ROWS, TILE), f32),
        pltpu.VMEM((16, ROWS, TILE), f32),
        pltpu.VMEM((2, ND, ROWS, TILE), f32),
        pltpu.VMEM((15, ROWS, TILE), f32),
        dma, dma((count,)), dma((count,)), dma((count,)), dma((count,)),
        dma((NZ - 1,)), dma((NZ - 1,)), dma((2,)), dma((2,)), dma((15,)), dma((15,)),
        dma((NZ - 1,)), dma((NZ - 1,)), dma((2,)), dma((2,)), dma((15,)), dma((15,)),
    ]
    density, potential = pl.pallas_call(
        kernel,
        out_shape=(
            jax.ShapeDtypeStruct(weights.shape, f32),
            jax.ShapeDtypeStruct(density_matrix.shape, f32),
        ),
        in_specs=[
            pl.BlockSpec(memory_space=pltpu.SMEM), vmem, pl.BlockSpec(memory_space=pl.ANY),
            vmem, vmem, vmem, vmem, vmem, vmem,
        ],
        out_specs=(vmem, vmem),
        scratch_shapes=scratch,
        compiler_params=pltpu.CompilerParams(
            collective_id=0, has_side_effects=True, vmem_limit_bytes=66_000_000
        ),
    )(
        union, density_matrix, basis, weights,
        in_scale[None], in_shift[None], hidden_weight, hidden_bias[None], out_weight[None],
    )
    return density, potential


def solution(mesh):
    own = P(("space", "dev"), None)
    in_specs = (own, P(("space", "dev"), None, None), own, own, P(), P(), P(), P(), P())
    return jax.shard_map(on_device, mesh=mesh, in_specs=in_specs, out_specs=(own, own), check_vma=False)
```

```python
import heapq

import jax
import jax.numpy as jnp
from jax import lax
from jax.experimental import pallas as pl
from jax.experimental.pallas import tpu as pltpu
from jax.sharding import PartitionSpec as P

MESH = pl.DeviceIdType.MESH
TILE = 128
U = 8
NX, NZ = 4, 8
NS = 8
ROWS = 16
REG = 4 * TILE
PB = 384
NP = 2 * PB

STRIPS = 16
FAR = 11
SHARED = STRIPS - FAR

CLASSES = (
    (FAR, STRIPS, True, 1),
    (0, 5, True, -1),
    (5, 8, False, 1),
    (8, FAR, False, -1),
)


def class_nodes(sign):
    xs = (0, 1, -1, 2 * sign)
    zs = (0, 1, -1, 2, -2, 3, -3, 4 * sign)
    return [(dx, dz) for dx in xs for dz in zs if (dx, dz) != (0, 0)]


def parent_of(node, z_first):
    dx, dz = node
    step_x = (dx > 0) - (dx < 0)
    step_z = (dz > 0) - (dz < 0)
    if z_first:
        return ((dx - step_x, dz), (step_x, 0)) if dx else ((0, dz - step_z), (0, step_z))
    return ((dx, dz - step_z), (0, step_z)) if dz else ((dx - step_x, 0), (step_x, 0))


def plan(latency=11.0, ahead=12.0):
    children = {}
    for c, (lo, hi, z_first, sign) in enumerate(CLASSES):
        for node in class_nodes(sign):
            par, step = parent_of(node, z_first)
            children.setdefault((c, par), []).append((c, node, step))

    def depth(c, node):
        return 1 + max((depth(c, kid[1]) for kid in children.get((c, node), [])), default=0)

    rank_z, rank_x = (0, 1, 2, 3), (2, 3, 0, 1)
    waiting = {}
    free = {}
    events = []
    issue = []
    arrive = {}
    count = 0

    def offer(now, kids):
        nonlocal count
        for c, node, step in kids:
            rank = (rank_z if step[1] else rank_x)[c]
            count += 1
            heapq.heappush(waiting.setdefault(step, []), (rank, -depth(c, node), count, now, c, node, step))
            count += 1
            heapq.heappush(events, (max(now, free.get(step, 0.0)), count, step, None))

    for c in range(len(CLASSES)):
        offer(0.0, children[(c, (0, 0))])
    while events:
        now, _, step, landed = heapq.heappop(events)
        if landed is not None:
            offer(now, children.get(landed, []))
            continue
        if free.get(step, 0.0) > now or not waiting[step]:
            continue
        _, _, _, ready, c, node, step = heapq.heappop(waiting[step])
        size = CLASSES[c][1] - CLASSES[c][0]
        free[step] = now + size
        arrive[(c, node)] = now + size + latency
        issue.append((max(ready, now - ahead), len(issue), c, node, step))
        count += 1
        heapq.heappush(events, (arrive[(c, node)], count, step, (c, node)))
        count += 1
        heapq.heappush(events, (free[step], count, step, None))
    return sorted(issue), arrive, children


ISSUE, ARRIVE, CHILDREN = plan()
STEP = {(c, node): step for _, _, c, node, step in ISSUE}
PARENT = {kid[:2]: par for par, kids in CHILDREN.items() for kid in kids}
BACK = sorted(STEP, key=lambda key: -ARRIVE[key])
NN = NX * NZ - 1
NODE_ID = {}
for _c in range(len(CLASSES)):
    for _k, _node in enumerate(class_nodes(CLASSES[_c][3])):
        NODE_ID[(_c, _node)] = _k
X_STEPS = (0, 1, -1, 2)


def split(value):
    high = value.astype(jnp.bfloat16)
    low = (value - high.astype(jnp.float32)).astype(jnp.bfloat16)
    return high, low


def swap_groups(parts):
    lane = lax.broadcasted_iota(jnp.int32, (ROWS, TILE), 1) // ROWS
    parts = list(parts)
    for bit in range(3):
        d = 1 << bit
        upper = (lane // d) % 2 == 1
        for i in range(8):
            if i & d:
                continue
            a, b = parts[i], parts[i + d]
            parts[i] = jnp.where(upper, pltpu.roll(b, ROWS * d, 1), a)
            parts[i + d] = jnp.where(upper, b, pltpu.roll(a, TILE - ROWS * d, 1))
    return parts


def fdot(a, b):
    return jnp.dot(a, b, preferred_element_type=jnp.float32)


def kernel(
    union_ref, rows_ref, basis_hbm, weights_ref, scale_ref, shift_ref, hidden_ref, bias_ref, out_w_ref,
    density_ref, potential_ref,
    basis_ref, full_ref, v3_ref, bth_ref, btl_ref, sh_ref, sl_ref, t3_ref, acc_ref, res_ref,
    gath_ref, gath2_ref, part_ref, part2_ref, land_ref, land2_ref,
    msend_ref, mrecv_ref, tt_ref, dsend_ref, dland_ref, tland_ref, mine_ref,
    msend2_ref, mrecv2_ref, ss_ref, dland2_ref, tland2_ref,
    basis_sem, ag_send, ag_recv, rs_send, rs_recv, pa_send, pa_recv, pr_send, pr_recv,
    m_send, m_recv, d_send, d_recv, t_send, t_recv,
    m2_send, m2_recv, d2_send, d2_recv, t2_send, t2_recv,
):
    region = lax.axis_index("space")
    dev = lax.axis_index("dev")
    x = dev // NZ
    z = dev % NZ
    core = region % 2
    sigma = 1 - 2 * core

    def at(offset):
        return (region + offset + 2 * NS) % NS

    outer, partner = at(-sigma), at(sigma)
    beyond = at(-2 * sigma)
    past = at(2 * sigma)

    def xof(d):
        return (x + d + 2 * NX) % NX

    def zof(d):
        return (z + d + 2 * NZ) % NZ

    def target(reg, xx, zz):
        return {"space": reg, "dev": xx * NZ + zz}

    load = pltpu.make_async_copy(basis_hbm, basis_ref, basis_sem)
    load.start()

    barrier = pltpu.get_barrier_semaphore()
    peers = [target(region, x, zof(d)) for d in range(1, NZ)]
    peers += [target(region, xof(d), z) for d in range(1, NX)]
    peers += [target(outer, xof(d), z) for d in range(NX)]
    peers += [target(partner, xof(d), z) for d in range(NX)]
    for peer in peers:
        pl.semaphore_signal(barrier, inc=1, device_id=peer, device_id_type=MESH)

    sent = []

    def remote(src, dst, send_sem, recv_sem, where):
        return pltpu.make_async_remote_copy(
            src_ref=src, dst_ref=dst, send_sem=send_sem, recv_sem=recv_sem,
            device_id=where, device_id_type=MESH,
        )

    def go(*args):
        copy = remote(*args)
        copy.start()
        sent.append(copy)

    def landed(slot, send_sem, recv_sem, where):
        remote(slot, slot, send_sem, recv_sem, where).wait_recv()

    def row_tile(reg, tile):
        return pl.ds(pl.multiple_of(reg * REG + tile * TILE, TILE), TILE)

    for d in range(3):
        strip = rows_ref[:, row_tile(region, xof(d))]
        dsend_ref[d] = strip
        mine_ref[FAR + d] = strip
    for j in range(4):
        dsend_ref[3 + j] = rows_ref[:, row_tile(outer, j)]
        dsend_ref[7 + j] = rows_ref[:, row_tile(beyond, j)]
    for e in range(2):
        mine_ref[FAR + 3 + e] = rows_ref[:, row_tile(partner, xof(core + e))]

    def transposed_columns():
        cols = [row_tile(region, xof(-1))]
        cols += [row_tile(outer, j) for j in range(4)]
        cols += [row_tile(past, j) for j in range(4)]
        cols += [row_tile(partner, xof(core - 1 - e)) for e in range(2)]
        return cols

    slots = [rows_ref[:, cols] for cols in transposed_columns()]
    zero = jnp.zeros((ROWS, TILE), jnp.float32)
    slots += [zero] * (16 - len(slots))
    for grp in range(2):
        for zz, part in enumerate(swap_groups(slots[8 * grp : 8 * grp + 8])):
            msend_ref[zz, grp] = part

    pl.semaphore_wait(barrier, len(peers))
    for k in range(1, NZ):
        go(msend_ref.at[zof(k)], mrecv_ref.at[z], m_send.at[k - 1], m_recv.at[k - 1], target(region, x, zof(k)))
    go(dsend_ref, dland_ref, d_send, d_recv, target(outer, x, z))
    mrecv_ref[z] = msend_ref[z]
    t3_ref[...] = jnp.zeros_like(t3_ref)
    acc_ref[...] = jnp.zeros_like(acc_ref)

    for k in range(1, NZ):
        landed(mrecv_ref.at[zof(-k)], m_send.at[k - 1], m_recv.at[k - 1], target(region, x, zof(k)))
    for grp in range(2):
        stacked = mrecv_ref[:, grp].reshape(TILE, TILE).T
        for e in range(8):
            tt_ref[8 * grp + e] = stacked[ROWS * e : ROWS * (e + 1)]

    kinds = [(0, outer, xof(-1), 1)]
    kinds += [(1 + xof(-d), region, xof(-d), 3 + xof(d)) for d in range(NX)]
    kinds += [(5 + xof(-d), partner, xof(-d), 7 + xof(d)) for d in range(NX)]
    kinds += [(0, region, xof(-1), FAR + 1)]
    kinds += [(9 + e, partner, xof(core - 1 - e), FAR + 3 + e) for e in range(2)]
    local = 1
    for k, (slot, reg, xx, _) in enumerate(kinds):
        if k == local:
            tland_ref[k] = tt_ref[slot]
        else:
            go(tt_ref.at[slot], tland_ref.at[k], t_send.at[k], t_recv.at[k], target(reg, xx, z))

    landed(dland_ref, d_send, d_recv, target(outer, x, z))
    mine_ref[0:FAR] = dland_ref[...]
    for k, (_, reg, xx, strip) in enumerate(kinds):
        if k != local:
            landed(tland_ref.at[k], t_send.at[k], t_recv.at[k], target(reg, xx, z))
        mine_ref[strip] += tland_ref[k]
    gath_ref[x, z] = mine_ref[...]

    beside = {
        step: target(region, xof(step[0]), zof(step[1])) for step in ((1, 0), (-1, 0), (0, 1), (0, -1))
    }
    against = {step: beside[(-step[0], -step[1])] for step in beside}
    other_core = target(partner, x, z)

    def block(ref, c, node):
        lo, hi = CLASSES[c][:2]
        return ref.at[xof(-node[0]), zof(-node[1]), lo:hi]

    done = {(c, (0, 0)) for c in range(len(CLASSES))}

    def need(c, node):
        if (c, node) not in done:
            done.add((c, node))
            view = block(gath_ref, c, node)
            sem = c * NN + NODE_ID[(c, node)]
            landed(view, ag_send.at[sem], ag_recv.at[sem], beside[STEP[(c, node)]])

    def need_class(c):
        for node in class_nodes(CLASSES[c][3]):
            need(c, node)

    def forward(c, node):
        par = PARENT[(c, node)]
        need(*par)
        view = block(gath_ref, c, par[1])
        sem = c * NN + NODE_ID[(c, node)]
        go(view, view, ag_send.at[sem], ag_recv.at[sem], beside[STEP[(c, node)]])

    def share(k):
        dx = X_STEPS[k]
        for node in [(dx, 0)] + [n for n in class_nodes(CLASSES[0][3]) if n[0] == dx and n[1] != 0]:
            need(0, node)
        go(gath_ref.at[xof(-dx), :, FAR:STRIPS], gath2_ref.at[xof(-dx)], pa_send.at[k], pa_recv.at[k], other_core)

    def shared(k):
        landed(gath2_ref.at[xof(-X_STEPS[k])], pa_send.at[k], pa_recv.at[k], other_core)

    slot_region = (outer, region, partner)

    def prepare(t):
        s, off = t // 4, (t % 4) * TILE
        tile = slot_region[s] * 4 + t % 4
        for b in range(2):
            value = None
            for u in range(U):
                hit = (union_ref[b, u] == tile).astype(jnp.float32)
                term = basis_ref[b, :, u * TILE : (u + 1) * TILE] * hit
                value = term if value is None else value + term
            high, low = split(value)
            rows = slice(b * PB, (b + 1) * PB)
            full_ref[rows, t * TILE : (t + 1) * TILE] = value
            for part, src in enumerate((high, low, high)):
                v3_ref[s, rows, REG * part + off : REG * part + off + TILE] = src
            high_t, low_t = split(value.T)
            bth_ref[t * TILE : (t + 1) * TILE, rows] = high_t
            btl_ref[t * TILE : (t + 1) * TILE, rows] = low_t

    def lanes(tile):
        return pl.ds(pl.multiple_of(tile * TILE, TILE), TILE)

    def unit_tiles(r, c):
        ref, base = ((gath_ref, 0), (gath_ref, FAR), (gath2_ref, 0))[r]
        for xx in range(NX):
            if r == c:
                yield from ((xx, slice((xx + d) % NX * TILE, ((xx + d) % NX + 1) * TILE), base + d) for d in range(3))
            elif r == 0:
                yield from ((xx, slice(j * TILE, (j + 1) * TILE), (3, 7)[c - 1] + j) for j in range(4))
            else:
                first = core if r == 1 else 1 - core
                yield from ((xx, lanes((xx + first + e) % NX), base + 3 + e) for e in range(2))

    def density_unit(r, c):
        ref = gath2_ref if r == 2 else gath_ref
        blank = jnp.zeros((TILE, TILE), jnp.bfloat16)

        def put(xx, cols, high, low):
            for part, src in enumerate((high, high, low)):
                t3_ref[REG * part + TILE * xx : REG * part + TILE * (xx + 1), cols] = src

        for xx, cols, strip in unit_tiles(r, c):
            put(xx, cols, *split(ref[xx, :, strip].reshape(TILE, TILE)))
        if r == c:
            for xx in range(NX):
                j = (xx + 3) % NX
                put(xx, slice(j * TILE, (j + 1) * TILE), blank, blank)
        elif r > 0:
            first = core if r == 1 else 1 - core
            for xx in range(NX):
                for e in (2, 3):
                    put(xx, lanes((xx + first + e) % NX), blank, blank)
        for q in range(2):
            res = fdot(v3_ref[r], t3_ref[:, 256 * q : 256 * (q + 1)])
            res = res * full_ref[:, REG * c + 256 * q : REG * c + 256 * (q + 1)]
            acc_ref[...] += res[:, :TILE] + res[:, TILE:]

    agenda = [(key, n, "send", (c, node)) for key, n, c, node, _ in ISSUE]
    for k, dx in enumerate(X_STEPS):
        key = max(ARRIVE[(0, n)] for n in class_nodes(CLASSES[0][3]) if n[0] == dx)
        agenda.append((key, k, "share", k))
    first_done, *ends = [max(ARRIVE[key] for key in STEP if key[0] == c) for c in range(len(CLASSES))]
    for t in range(12):
        agenda.append((4.0 + t * (first_done - 8.0) / 12, t, "prepare", (4, 5, 6, 7, 8, 9, 10, 11, 0, 1, 2, 3)[t]))
    agenda.append((first_done + 0.1, 0, "unit", (1, 1)))
    agenda.append((first_done + 10, 1, "unit", (1, 2)))
    agenda.append((first_done + 20, 2, "unit", (2, 1)))
    agenda.append((first_done + 30, 3, "unit", (2, 2)))
    for key, _, what, arg in sorted(agenda, key=lambda a: (a[0], a[2], a[1])):
        if what == "send":
            forward(*arg)
        elif what == "share":
            share(arg)
        elif what == "prepare":
            if arg == 4:
                load.wait()
            prepare(arg)
        else:
            if arg == (1, 1):
                need_class(0)
            if arg == (2, 1):
                for k in range(len(X_STEPS)):
                    shared(k)
            density_unit(*arg)
    if ends[2] < ends[0]:
        need_class(2)
        need_class(3)
        density_unit(0, 2)
        need_class(1)
    else:
        need_class(1)
        density_unit(0, 0)
        need_class(2)
        density_unit(0, 1)
        need_class(3)
        density_unit(0, 2)
    if ends[2] < ends[0]:
        density_unit(0, 0)
        density_unit(0, 1)
    rho = jnp.sum(acc_ref[...], axis=1, keepdims=True)

    hid_high, hid_low = split(hidden_ref[...])
    first = jnp.tanh(rho * scale_ref[...] + shift_ref[...])
    high, low = split(first)
    pre = fdot(high, hid_high) + fdot(low, hid_high) + fdot(high, hid_low) + bias_ref[...]
    second = pre / (1.0 + jnp.exp(-pre))
    pot = jnp.sum(second * out_w_ref[...], axis=1, keepdims=True)
    factors = []
    for b in range(2):
        rho_b = jnp.broadcast_to(rho[b * PB : (b + 1) * PB], (PB, TILE)).T
        density_ref[b : b + 1, :] = rho_b[0:1]
        w_b = jnp.broadcast_to(weights_ref[b : b + 1, :], (TILE, PB)).T
        factors.append(w_b[:, 0:1] * pot[b * PB : (b + 1) * PB])

    def scale_slot(s):
        for b in range(2):
            rows = slice(b * PB, (b + 1) * PB)
            for j in range(4):
                cols = slice(REG * s + TILE * j, REG * s + TILE * (j + 1))
                high, low = split(full_ref[rows, cols] * factors[b])
                sh_ref[rows, cols] = high
                sl_ref[rows, cols] = low

    def part_unit(r, c):
        rows = slice(REG * r, REG * (r + 1))
        ref = part2_ref if r == 2 else part_ref
        for q in range(2):
            cols = slice(REG * c + 256 * q, REG * c + 256 * (q + 1))
            right = sh_ref[:, cols]
            res_ref[:, 256 * q : 256 * (q + 1)] = (
                fdot(bth_ref[rows], right) + fdot(btl_ref[rows], right) + fdot(bth_ref[rows], sl_ref[:, cols])
            )
        for xx, cols, strip in unit_tiles(r, c):
            ref[xx, :, strip] = res_ref[TILE * xx : TILE * (xx + 1), cols].reshape(NZ, ROWS, TILE)

    def summed(c, node):
        lo, hi = CLASSES[c][:2]
        bx, bz = xof(-node[0]), zof(-node[1])
        if c == 0:
            if node[0] not in merged:
                merged.add(node[0])
                k = X_STEPS.index(node[0])
                landed(land2_ref.at[bx], pr_send.at[k], pr_recv.at[k], other_core)
            part_ref[bx, bz, lo:hi] += land2_ref[bx, bz]
        for _, kid, step in CHILDREN.get((c, node), []):
            k = NODE_ID[(c, kid)]
            sem = c * NN + k
            landed(land_ref.at[k, lo:hi], rs_send.at[sem], rs_recv.at[sem], against[step])
            part_ref[bx, bz, lo:hi] += land_ref[k, lo:hi]

    merged = set()

    def back(c, node):
        summed(c, node)
        lo, hi = CLASSES[c][:2]
        k = NODE_ID[(c, node)]
        go(
            block(part_ref, c, node), land_ref.at[k, lo:hi],
            rs_send.at[c * NN + k], rs_recv.at[c * NN + k], against[STEP[(c, node)]],
        )

    scale_slot(0)
    part_unit(0, 0)
    scale_slot(1)
    part_unit(0, 1)
    scale_slot(2)
    part_unit(0, 2)
    near = [key for key in BACK if key[0] == 0]
    start = BACK.index(near[0])
    marks = {min(start, 12): "partner", min(start, 30): "own"}
    for n, key in enumerate(BACK):
        what = marks.get(n)
        if what == "partner":
            part_unit(2, 2)
            part_unit(2, 1)
            for k in reversed(range(len(X_STEPS))):
                bx = xof(-X_STEPS[k])
                go(part2_ref.at[bx], land2_ref.at[bx], pr_send.at[k], pr_recv.at[k], other_core)
        elif what == "own":
            part_unit(1, 1)
            part_unit(1, 2)
        back(*key)

    own = part_ref.at[x, z]
    for c in (1, 2, 3):
        summed(c, (0, 0))
    go(own.at[0:FAR], dland2_ref, d2_send, d2_recv, target(outer, x, z))
    returns = [(1, outer, xof(1), 0)]
    returns += [(3 + xof(d), region, xof(d), 1 + xof(-d)) for d in range(NX)]
    returns += [(7 + xof(d), partner, xof(d), 5 + xof(-d)) for d in range(NX)]
    returns += [(FAR + 1, region, xof(1), 0)]
    returns += [(FAR + 3 + e, partner, xof(core + e), 9 + e) for e in range(2)]

    def give(k):
        strip, reg, xx, slot = returns[k]
        if k != local:
            go(own.at[strip], tland2_ref.at[k], t2_send.at[k], t2_recv.at[k], target(reg, xx, z))

    for k in range(9):
        give(k)
    summed(0, (0, 0))
    for k in range(9, 12):
        give(k)
    ss_ref[...] = jnp.zeros_like(ss_ref)
    for k, (strip, reg, xx, slot) in enumerate(returns):
        if k == local:
            ss_ref[slot] += part_ref[x, z, strip]
        else:
            landed(tland2_ref.at[k], t2_send.at[k], t2_recv.at[k], target(reg, xx, z))
            ss_ref[slot] += tland2_ref[k]
    for grp in range(2):
        stacked = ss_ref[8 * grp : 8 * grp + 8].reshape(TILE, TILE).T
        for zz in range(NZ):
            msend2_ref[zz, grp] = stacked[ROWS * zz : ROWS * (zz + 1)]
    for k in range(1, NZ):
        go(msend2_ref.at[zof(k)], mrecv2_ref.at[z], m2_send.at[k - 1], m2_recv.at[k - 1], target(region, x, zof(k)))
    mrecv2_ref[z] = msend2_ref[z]

    potential_ref[...] = jnp.zeros_like(potential_ref)
    for d in range(3):
        potential_ref[:, row_tile(region, xof(d))] += part_ref[x, z, FAR + d]
    for e in range(2):
        potential_ref[:, row_tile(partner, xof(core + e))] += part_ref[x, z, FAR + 3 + e]
    landed(dland2_ref, d2_send, d2_recv, target(outer, x, z))
    for d in range(3):
        potential_ref[:, row_tile(region, xof(d))] += dland2_ref[d]
    for j in range(4):
        potential_ref[:, row_tile(outer, j)] += dland2_ref[3 + j]
        potential_ref[:, row_tile(beyond, j)] += dland2_ref[7 + j]
    for k in range(1, NZ):
        landed(mrecv2_ref.at[zof(-k)], m2_send.at[k - 1], m2_recv.at[k - 1], target(region, x, zof(k)))
    turned = []
    for grp in range(2):
        turned += swap_groups([mrecv2_ref[zz, grp] for zz in range(NZ)])
    for e, cols in enumerate(transposed_columns()):
        potential_ref[:, cols] += turned[e]

    for copy in sent:
        copy.wait_send()


def on_device(density_matrix, basis, union, weights, in_scale, in_shift, hidden_weight, hidden_bias, out_weight):
    vmem = pl.BlockSpec(memory_space=pltpu.VMEM)
    f32, bf16 = jnp.float32, jnp.bfloat16
    dma = pltpu.SemaphoreType.DMA
    count = len(CLASSES) * NN
    strip = (ROWS, TILE)
    scratch = [
        pltpu.VMEM((2, PB, U * TILE), f32),
        pltpu.VMEM((NP, 3 * REG), f32),
        pltpu.VMEM((3, NP, 3 * REG), bf16),
        pltpu.VMEM((3 * REG, NP), bf16),
        pltpu.VMEM((3 * REG, NP), bf16),
        pltpu.VMEM((NP, 3 * REG), bf16),
        pltpu.VMEM((NP, 3 * REG), bf16),
        pltpu.VMEM((3 * REG, REG), bf16),
        pltpu.VMEM((NP, TILE), f32),
        pltpu.VMEM((REG, REG), f32),
        pltpu.VMEM((NX, NZ, STRIPS) + strip, f32),
        pltpu.VMEM((NX, NZ, SHARED) + strip, f32),
        pltpu.VMEM((NX, NZ, STRIPS) + strip, f32),
        pltpu.VMEM((NX, NZ, SHARED) + strip, f32),
        pltpu.VMEM((NN, STRIPS) + strip, f32),
        pltpu.VMEM((NX, NZ, SHARED) + strip, f32),
        pltpu.VMEM((NZ, 2) + strip, f32),
        pltpu.VMEM((NZ, 2) + strip, f32),
        pltpu.VMEM((16,) + strip, f32),
        pltpu.VMEM((FAR,) + strip, f32),
        pltpu.VMEM((FAR,) + strip, f32),
        pltpu.VMEM((12,) + strip, f32),
        pltpu.VMEM((STRIPS,) + strip, f32),
        pltpu.VMEM((NZ, 2) + strip, f32),
        pltpu.VMEM((NZ, 2) + strip, f32),
        pltpu.VMEM((16,) + strip, f32),
        pltpu.VMEM((FAR,) + strip, f32),
        pltpu.VMEM((12,) + strip, f32),
        dma, dma((count,)), dma((count,)), dma((count,)), dma((count,)),
        dma((4,)), dma((4,)), dma((4,)), dma((4,)),
        dma((NZ - 1,)), dma((NZ - 1,)), dma, dma, dma((12,)), dma((12,)),
        dma((NZ - 1,)), dma((NZ - 1,)), dma, dma, dma((12,)), dma((12,)),
    ]
    density, potential = pl.pallas_call(
        kernel,
        out_shape=(
            jax.ShapeDtypeStruct(weights.shape, f32),
            jax.ShapeDtypeStruct(density_matrix.shape, f32),
        ),
        in_specs=[
            pl.BlockSpec(memory_space=pltpu.SMEM), vmem, pl.BlockSpec(memory_space=pl.ANY),
            vmem, vmem, vmem, vmem, vmem, vmem,
        ],
        out_specs=(vmem, vmem),
        scratch_shapes=scratch,
        compiler_params=pltpu.CompilerParams(
            collective_id=0, has_side_effects=True, vmem_limit_bytes=66_000_000
        ),
    )(
        union, density_matrix, basis, weights,
        in_scale[None], in_shift[None], hidden_weight, hidden_bias[None], out_weight[None],
    )
    return density, potential


def solution(mesh):
    own = P(("space", "dev"), None)
    in_specs = (own, P(("space", "dev"), None, None), own, own, P(), P(), P(), P(), P())
    return jax.shard_map(on_device, mesh=mesh, in_specs=in_specs, out_specs=(own, own), check_vma=False)
```

```python
import heapq

import jax
import jax.numpy as jnp
from jax import lax
from jax.experimental import pallas as pl
from jax.experimental.pallas import tpu as pltpu
from jax.sharding import PartitionSpec as P

MESH = pl.DeviceIdType.MESH
TILE = 128
U = 8
NX, NZ = 4, 8
NS = 8
ROWS = 16
REG = 4 * TILE
PB = 384
NP = 2 * PB

STRIPS = 11
SHARED = 5
TO_PARTNER = (0, 5)
TO_OUTER = (2, 7)

CLASSES = (
    (0, 4, True, 1),
    (4, 7, True, -1),
    (7, 11, False, -1),
)
LATE = 10.0


def class_nodes(sign):
    xs = (0, 1, -1, 2 * sign)
    zs = (0, 1, -1, 2, -2, 3, -3, 4 * sign)
    return [(dx, dz) for dx in xs for dz in zs if (dx, dz) != (0, 0)]


def parent_of(node, z_first):
    dx, dz = node
    step_x = (dx > 0) - (dx < 0)
    step_z = (dz > 0) - (dz < 0)
    if z_first:
        return ((dx - step_x, dz), (step_x, 0)) if dx else ((0, dz - step_z), (0, step_z))
    return ((dx, dz - step_z), (0, step_z)) if dz else ((dx - step_x, 0), (step_x, 0))


def plan(latency=11.0, ahead=12.0):
    children = {}
    for c, (lo, hi, z_first, sign) in enumerate(CLASSES):
        for node in class_nodes(sign):
            par, step = parent_of(node, z_first)
            children.setdefault((c, par), []).append((c, node, step))

    def depth(c, node):
        return 1 + max((depth(c, kid[1]) for kid in children.get((c, node), [])), default=0)

    waiting = {}
    free = {}
    events = []
    issue = []
    arrive = {}
    count = 0

    def offer(now, kids):
        nonlocal count
        for c, node, step in kids:
            if step[1]:
                rank = (0, 1, 2)[c]
            else:
                rank = (1, 1, 0)[c] + (abs(node[0]) > 1)
            count += 1
            heapq.heappush(waiting.setdefault(step, []), (rank, -depth(c, node), count, now, c, node, step))
            count += 1
            heapq.heappush(events, (max(now, free.get(step, 0.0)), count, step, None))

    for c in range(len(CLASSES)):
        count += 1
        heapq.heappush(events, (LATE if c == 2 else 0.0, count, None, (c, (0, 0))))
    while events:
        now, _, step, landed = heapq.heappop(events)
        if landed is not None:
            offer(now, children.get(landed, []))
            continue
        if free.get(step, 0.0) > now or not waiting[step]:
            continue
        _, _, _, ready, c, node, step = heapq.heappop(waiting[step])
        size = CLASSES[c][1] - CLASSES[c][0]
        free[step] = now + size
        arrive[(c, node)] = now + size + latency
        issue.append((max(ready, now - ahead), len(issue), c, node, step))
        count += 1
        heapq.heappush(events, (arrive[(c, node)], count, step, (c, node)))
        count += 1
        heapq.heappush(events, (free[step], count, step, None))
    return sorted(issue), arrive, children


ISSUE, ARRIVE, CHILDREN = plan()
STEP = {(c, node): step for _, _, c, node, step in ISSUE}
PARENT = {kid[:2]: par for par, kids in CHILDREN.items() for kid in kids}
BACK = sorted(STEP, key=lambda key: -ARRIVE[key])
NN = NX * NZ - 1
NODE_ID = {}
NODE_AT = {}
for _c in range(len(CLASSES)):
    NODE_AT[(_c, 0, 0)] = (0, 0)
    for _k, _node in enumerate(class_nodes(CLASSES[_c][3])):
        NODE_ID[(_c, _node)] = _k
        NODE_AT[(_c, _node[0] % NX, _node[1] % NZ)] = _node
PAIRS = ((0, 1), (3, 2))


def split(value):
    high = value.astype(jnp.bfloat16)
    low = (value - high.astype(jnp.float32)).astype(jnp.bfloat16)
    return high, low


def swap_groups(parts):
    lane = lax.broadcasted_iota(jnp.int32, (ROWS, TILE), 1) // ROWS
    parts = list(parts)
    for bit in range(3):
        d = 1 << bit
        upper = (lane // d) % 2 == 1
        for i in range(8):
            if i & d:
                continue
            a, b = parts[i], parts[i + d]
            parts[i] = jnp.where(upper, pltpu.roll(b, ROWS * d, 1), a)
            parts[i + d] = jnp.where(upper, b, pltpu.roll(a, TILE - ROWS * d, 1))
    return parts


def fdot(a, b):
    return jnp.dot(a, b, preferred_element_type=jnp.float32)


def kernel(
    union_ref, rows_hbm, basis_hbm, weights_hbm, scale_hbm, shift_hbm, hidden_hbm, bias_hbm, out_w_hbm,
    density_ref, potential_ref,
    rows_ref, basis_ref, weights_ref, scale_ref, shift_ref, hidden_ref, bias_ref, out_w_ref,
    full_ref, v3_ref, bth_ref, btl_ref, sh_ref, sl_ref, t3_ref, acc_ref, res_ref,
    gath_ref, gath2_ref, gath0_ref, part_ref, part2_ref, part0_ref, land_ref, land2_ref, land0_ref,
    msend_ref, mrecv_ref, turn_ref, dland_ref, pland_ref,
    msend2_ref, mrecv2_ref, ss_ref, dland2_ref, pland2_ref,
    load_sem, ag_send, ag_recv, rs_send, rs_recv,
    pa_send, pa_recv, pr_send, pr_recv, oa_send, oa_recv, or_send, or_recv,
    m_send, m_recv, d_send, d_recv, p_send, p_recv,
    m2_send, m2_recv, d2_send, d2_recv, p2_send, p2_recv,
):
    region = lax.axis_index("space")
    dev = lax.axis_index("dev")
    x = dev // NZ
    z = dev % NZ
    core = region % 2
    sigma = 1 - 2 * core

    def at(offset):
        return (region + offset + 2 * NS) % NS

    outer, partner = at(-sigma), at(sigma)
    beyond = at(-2 * sigma)
    past = at(2 * sigma)

    def xof(d):
        return (x + d + 2 * NX) % NX

    def zof(d):
        return (z + d + 2 * NZ) % NZ

    def target(reg, xx, zz):
        return {"space": reg, "dev": xx * NZ + zz}

    loads = []
    for k, (src, dst) in enumerate(
        (
            (rows_hbm, rows_ref), (basis_hbm, basis_ref), (weights_hbm, weights_ref), (scale_hbm, scale_ref),
            (shift_hbm, shift_ref), (hidden_hbm, hidden_ref), (bias_hbm, bias_ref), (out_w_hbm, out_w_ref),
        )
    ):
        copy = pltpu.make_async_copy(src, dst, load_sem.at[k])
        copy.start()
        loads.append(copy)

    barrier = pltpu.get_barrier_semaphore()
    peers = [target(region, x, zof(d)) for d in range(1, NZ)]
    peers += [target(region, xof(d), z) for d in range(1, NX)]
    peers += [target(outer, xof(d), z) for d in range(NX)]
    peers += [target(partner, xof(d), z) for d in range(NX)]
    for peer in peers:
        pl.semaphore_signal(barrier, inc=1, device_id=peer, device_id_type=MESH)

    sent = []

    def remote(src, dst, send_sem, recv_sem, where):
        return pltpu.make_async_remote_copy(
            src_ref=src, dst_ref=dst, send_sem=send_sem, recv_sem=recv_sem,
            device_id=where, device_id_type=MESH,
        )

    def go(*args):
        copy = remote(*args)
        copy.start()
        sent.append(copy)

    def landed(slot, send_sem, recv_sem, where):
        remote(slot, slot, send_sem, recv_sem, where).wait_recv()

    def row_tile(reg, tile):
        return pl.ds(pl.multiple_of(reg * REG + tile * TILE, TILE), TILE)

    own_cols = [row_tile(region, xof(1))]
    own_cols += [row_tile(partner, xof(core + e)) for e in range(2)]
    own_cols += [row_tile(outer, xof(core + e)) for e in range(2)]
    past_cols = [row_tile(past, i) for i in range(NX)]
    loads[0].wait()
    zero = jnp.zeros((ROWS, TILE), jnp.float32)
    for grp, cols in enumerate((own_cols, past_cols)):
        slots = [rows_ref[:, c] for c in cols]
        for zz, part in enumerate(swap_groups(slots + [zero] * (8 - len(slots)))):
            msend_ref[grp, zz] = part

    pl.semaphore_wait(barrier, len(peers))
    for grp in range(2):
        for k in range(1, NZ):
            go(
                msend_ref.at[grp, zof(k)], mrecv_ref.at[grp, z], m_send.at[grp, k - 1], m_recv.at[grp, k - 1],
                target(region, x, zof(k)),
            )
        if grp == 0:
            direct = [(region, xof(-1), row_tile(region, xof(-1)), 0), (region, xof(-2), row_tile(region, xof(-2)), 1)]
            direct += [(partner, xof(core - 1 - e), row_tile(partner, xof(core - 1 - e)), 2 + e) for e in range(2)]
            direct += [(outer, xof(core - 1 - e), row_tile(outer, xof(core - 1 - e)), 4 + e) for e in range(2)]
            direct += [(outer, xof(d), row_tile(beyond, xof(d)), 6 + x) for d in range(NX)]
            for k, (reg, xx, cols, slot) in enumerate(direct):
                go(rows_ref.at[:, cols], dland_ref.at[slot], d_send.at[k], d_recv.at[k], target(reg, xx, z))
    for grp in range(2):
        mrecv_ref[grp, z] = msend_ref[grp, z]

    def arrived(k):
        slot = k if k < 6 else 6 + xof(-(k - 6))
        reg, xx = direct[k][:2]
        landed(dland_ref.at[slot], d_send.at[k], d_recv.at[k], target(reg, xx, z))

    def turned_in(grp):
        for k in range(1, NZ):
            landed(
                mrecv_ref.at[grp, zof(-k)], m_send.at[grp, k - 1], m_recv.at[grp, k - 1], target(region, x, zof(k))
            )
        return mrecv_ref[grp].reshape(TILE, TILE).T

    acc_ref[...] = jnp.zeros_like(acc_ref)
    turned = turned_in(0)

    def turned_strip(e):
        return turned[ROWS * e : ROWS * (e + 1)]

    for k in range(6):
        arrived(k)
    gath_ref[x, z, 2] = rows_ref[:, row_tile(region, x)]
    gath_ref[x, z, 3] = dland_ref[0] + turned_strip(0)
    gath_ref[x, z, 4] = dland_ref[1]
    for e in range(2):
        gath_ref[x, z, e] = dland_ref[2 + e] + turned_strip(1 + e)
        gath_ref[x, z, 5 + e] = dland_ref[4 + e] + turned_strip(3 + e)

    beside = {
        step: target(region, xof(step[0]), zof(step[1])) for step in ((1, 0), (-1, 0), (0, 1), (0, -1))
    }
    against = {step: beside[(-step[0], -step[1])] for step in beside}
    other_core = target(partner, x, z)
    other_chip = target(outer, x, z)

    def block(ref, c, node):
        lo, hi = CLASSES[c][:2]
        return ref.at[xof(-node[0]), zof(-node[1]), lo:hi]

    done = {(c, (0, 0)) for c in range(len(CLASSES))}

    def need(c, node):
        if (c, node) not in done:
            done.add((c, node))
            view = block(gath_ref, c, node)
            sem = c * NN + NODE_ID[(c, node)]
            landed(view, ag_send.at[sem], ag_recv.at[sem], beside[STEP[(c, node)]])

    def forward(c, node):
        par = PARENT[(c, node)]
        need(*par)
        view = block(gath_ref, c, par[1])
        sem = c * NN + NODE_ID[(c, node)]
        go(view, view, ag_send.at[sem], ag_recv.at[sem], beside[STEP[(c, node)]])

    def need_block(ax, az):
        need(0, NODE_AT[(0, ax, az)])
        need(1, NODE_AT[(1, ax, az)])

    def to_partner(ax):
        for az in range(NZ):
            need_block(ax, az)
        bx = xof(-ax)
        lo, hi = TO_PARTNER
        go(gath_ref.at[bx, :, lo:hi], gath2_ref.at[bx], pa_send.at[ax], pa_recv.at[ax], other_core)

    def to_outer(ax, az):
        need_block(ax, az)
        bx, bz = xof(-ax), zof(-az)
        lo, hi = TO_OUTER
        k = ax * NZ + az
        go(gath_ref.at[bx, bz, lo:hi], gath0_ref.at[bx, bz], oa_send.at[k], oa_recv.at[k], other_chip)

    def from_partner(ax):
        landed(gath2_ref.at[xof(-ax)], pa_send.at[ax], pa_recv.at[ax], other_core)

    def from_outer(ax, az):
        k = ax * NZ + az
        landed(gath0_ref.at[xof(-ax), zof(-az)], oa_send.at[k], oa_recv.at[k], other_chip)

    def start_late():
        late = turned_in(1)
        for i in range(NX):
            turn_ref[i] = late[ROWS * i : ROWS * (i + 1)]
        go(turn_ref, pland_ref, p_send, p_recv, other_core)
        for k in range(6, 10):
            arrived(k)
        landed(pland_ref, p_send, p_recv, other_core)
        gath_ref[x, z, 7:11] = dland_ref[6:10] + pland_ref[...]

    slot_region = (outer, region, partner)

    def prepare(t):
        s, off = t // 4, (t % 4) * TILE
        tile = slot_region[s] * 4 + t % 4
        for b in range(2):
            value = None
            for u in range(U):
                hit = (union_ref[b, u] == tile).astype(jnp.float32)
                term = basis_ref[b, :, u * TILE : (u + 1) * TILE] * hit
                value = term if value is None else value + term
            high, low = split(value)
            rows = slice(b * PB, (b + 1) * PB)
            full_ref[rows, t * TILE : (t + 1) * TILE] = value
            for part, src in enumerate((high, low, high)):
                v3_ref[s, rows, REG * part + off : REG * part + off + TILE] = src
            high_t, low_t = split(value.T)
            bth_ref[t * TILE : (t + 1) * TILE, rows] = high_t
            btl_ref[t * TILE : (t + 1) * TILE, rows] = low_t

    def span(base, tile):
        return pl.ds(pl.multiple_of(base + tile * TILE, TILE), TILE)

    def unit_tiles(r, c, xx):
        if r == c:
            base = (0, 2, 2)[r]
            return [((xx + d) % NX, base + d) for d in range(3)], [(xx + 3) % NX]
        if (r, c) == (0, 2):
            return [(i, 7 + i) for i in range(NX)], []
        first = core if c == 1 else 1 - core
        base = {(2, 1): 0, (0, 1): 5, (1, 2): 0, (1, 0): 3}[(r, c)]
        return (
            [((xx + first + e) % NX, base + e) for e in range(2)],
            [(xx + first + e) % NX for e in (2, 3)],
        )

    UNITS = ((1, 1), (2, 1), (0, 1), (2, 2), (1, 2), (0, 0), (1, 0), (0, 2))

    def holder(r, c, own, partners, outers):
        if c == 1 or (r, c) == (0, 2):
            return own
        return partners if c == 2 else outers

    def density_unit(r, c, pair):
        ref = holder(r, c, gath_ref, gath2_ref, gath0_ref)
        blank = jnp.zeros((TILE, TILE), jnp.bfloat16)

        def fill(h, carry):
            xx = xof(-pair[0] - h * (pair[1] - pair[0]))
            held, absent = unit_tiles(r, c, xx)
            cols = span(0, h)
            for row, strip in held:
                high, low = split(ref[xx, :, strip].reshape(TILE, TILE))
                for part, src in enumerate((high, high, low)):
                    t3_ref[span(REG * part, row), cols] = src
            for row in absent:
                for part in range(3):
                    t3_ref[span(REG * part, row), cols] = blank
            return carry

        lax.fori_loop(0, 2, fill, 0)
        res = fdot(v3_ref[r], t3_ref[...])
        for h, ax in enumerate(pair):
            other = full_ref[:, span(REG * c, xof(-ax))]
            acc_ref[...] += res[:, h * TILE : (h + 1) * TILE] * other

    agenda = [(key, n, "send", (c, node)) for key, n, c, node, _ in ISSUE]
    landing = {}
    for ax in range(NX):
        for az in range(NZ):
            landing[(ax, az)] = max(ARRIVE.get((c, NODE_AT[(c, ax, az)]), 0.0) for c in range(2))
            agenda.append((landing[(ax, az)], NZ * ax + az, "outer", (ax, az)))
        agenda.append((max(landing[(ax, az)] for az in range(NZ)) + 0.1, ax, "partner", (ax,)))
    pair_end = max(landing[(ax, az)] for ax in PAIRS[0] for az in range(NZ))
    order = (4, 5, 6, 7, 8, 9, 10, 11, 0, 1, 2, 3)
    for t in range(12):
        agenda.append((6.0 + t * (pair_end - 14.0) / 12, t, "prepare", (order[t],)))
    for n, unit in enumerate(UNITS[:7]):
        agenda.append((pair_end + 1 + 6 * n + (8 if n > 2 else 0) + (8 if n > 4 else 0), n, "unit", unit))
    agenda.append((LATE - 0.5, 0, "late", ()))
    got_partner, got_outer = set(), set()

    def unit_ready(r, c, pair):
        if (r, c) == (0, 2):
            for node in class_nodes(CLASSES[2][3]):
                need(2, node)
            return
        for ax in pair:
            if c == 1:
                for az in range(NZ):
                    need_block(ax, az)
            elif c == 2 and ax not in got_partner:
                got_partner.add(ax)
                from_partner(ax)
            elif c == 0 and ax not in got_outer:
                got_outer.add(ax)
                for az in range(NZ):
                    from_outer(ax, az)

    for key, _, what, arg in sorted(agenda, key=lambda a: (a[0], a[2], a[1])):
        if what == "send":
            forward(*arg)
        elif what == "late":
            start_late()
        elif what == "outer":
            to_outer(*arg)
        elif what == "partner":
            to_partner(*arg)
        elif what == "prepare":
            if arg[0] == order[0]:
                loads[1].wait()
            prepare(*arg)
        else:
            unit_ready(*arg, PAIRS[0])
            density_unit(*arg, PAIRS[0])
    for r, c in UNITS:
        for pair in PAIRS:
            if pair == PAIRS[1] or (r, c) == UNITS[7]:
                unit_ready(r, c, pair)
                density_unit(r, c, pair)
    rho = jnp.sum(acc_ref[...], axis=1, keepdims=True)

    for copy in loads[2:]:
        copy.wait()
    hid_high, hid_low = split(hidden_ref[...])
    first = jnp.tanh(rho * scale_ref[...] + shift_ref[...])
    high, low = split(first)
    pre = fdot(high, hid_high) + fdot(low, hid_high) + fdot(high, hid_low) + bias_ref[...]
    second = pre / (1.0 + jnp.exp(-pre))
    pot = jnp.sum(second * out_w_ref[...], axis=1, keepdims=True)
    factors = []
    for b in range(2):
        rho_b = jnp.broadcast_to(rho[b * PB : (b + 1) * PB], (PB, TILE)).T
        density_ref[b : b + 1, :] = rho_b[0:1]
        w_b = jnp.broadcast_to(weights_ref[b : b + 1, :], (TILE, PB)).T
        factors.append(w_b[:, 0:1] * pot[b * PB : (b + 1) * PB])

    def scale_slot(s):
        for b in range(2):
            rows = slice(b * PB, (b + 1) * PB)
            for j in range(4):
                cols = slice(REG * s + TILE * j, REG * s + TILE * (j + 1))
                high, low = split(full_ref[rows, cols] * factors[b])
                sh_ref[rows, cols] = high
                sl_ref[rows, cols] = low

    def part_unit(r, c, pair):
        rows = slice(REG * r, REG * (r + 1))
        ref = holder(r, c, part_ref, part2_ref, part0_ref)
        tiles = [xof(-ax) for ax in pair]
        right = jnp.concatenate([sh_ref[:, span(REG * c, xx)] for xx in tiles], axis=1)
        right_low = jnp.concatenate([sl_ref[:, span(REG * c, xx)] for xx in tiles], axis=1)
        res_ref[...] = fdot(bth_ref[rows], right) + fdot(btl_ref[rows], right) + fdot(bth_ref[rows], right_low)
        for h, xx in enumerate(tiles):
            for row, strip in unit_tiles(r, c, xx)[0]:
                ref[xx, :, strip] = res_ref[span(0, row), h * TILE : (h + 1) * TILE].reshape(NZ, ROWS, TILE)

    back_partner, back_outer = set(), set()

    def summed(c, node):
        lo, hi = CLASSES[c][:2]
        ax, az = node[0] % NX, node[1] % NZ
        bx, bz = xof(-ax), zof(-az)
        if c < 2:
            if ax not in back_partner:
                back_partner.add(ax)
                landed(land2_ref.at[bx], pr_send.at[ax], pr_recv.at[ax], other_core)
            if (ax, az) not in back_outer:
                back_outer.add((ax, az))
                k = ax * NZ + az
                landed(land0_ref.at[bx, bz], or_send.at[k], or_recv.at[k], other_chip)
        kids = CHILDREN.get((c, node), [])
        for _, kid, step in kids:
            sem = c * NN + NODE_ID[(c, kid)]
            slot = land_ref.at[NODE_ID[(c, kid)], lo:hi]
            landed(slot, rs_send.at[sem], rs_recv.at[sem], against[step])

        def add(i, carry):
            rows = pl.ds(pl.multiple_of(8 * i, 8), 8)
            total = part_ref[bx, bz, lo:hi, rows]
            for _, kid, _ in kids:
                total = total + land_ref[NODE_ID[(c, kid)], lo:hi, rows]
            part_ref[bx, bz, lo:hi, rows] = total
            if c < 2:
                for ref, (first, last) in ((land2_ref, TO_PARTNER), (land0_ref, TO_OUTER)):
                    a, b = max(lo, first), min(hi, last)
                    part_ref[bx, bz, a:b, rows] += ref[bx, bz, a - first : b - first, rows]
            return carry

        if c < 2 or kids:
            lax.fori_loop(0, ROWS // 8, add, 0)

    def back(c, node):
        summed(c, node)
        lo, hi = CLASSES[c][:2]
        k = NODE_ID[(c, node)]
        go(
            block(part_ref, c, node), land_ref.at[k, lo:hi],
            rs_send.at[c * NN + k], rs_recv.at[c * NN + k], against[STEP[(c, node)]],
        )

    def back_to_outer(pair):
        for ax, az in sorted(landing, key=lambda b: -landing[b]):
            if ax in pair:
                bx, bz = xof(-ax), zof(-az)
                k = ax * NZ + az
                go(part0_ref.at[bx, bz], land0_ref.at[bx, bz], or_send.at[k], or_recv.at[k], other_chip)

    def back_to_partner(pair):
        for ax in reversed(pair):
            bx = xof(-ax)
            go(part2_ref.at[bx], land2_ref.at[bx], pr_send.at[ax], pr_recv.at[ax], other_core)

    first_pair, last_pair = PAIRS[1], PAIRS[0]
    scale_slot(0)
    part_unit(0, 0, first_pair)
    part_unit(1, 0, first_pair)
    back_to_outer(first_pair)
    scale_slot(2)
    part_unit(0, 2, first_pair)
    part_unit(0, 2, last_pair)
    near = [key for key in BACK if key[0] < 2]
    far = [key for key in BACK if key[0] == 2]
    for key in far[:8]:
        back(*key)
    rest = [key for key in BACK if key not in far[:8]]
    part_unit(2, 2, first_pair)
    part_unit(1, 2, first_pair)
    back_to_partner(first_pair)
    scale_slot(1)
    for r, c in UNITS[:3]:
        part_unit(r, c, first_pair)
    todo = [
        [((0, 0), (1, 0)), back_to_outer],
        [((2, 2), (1, 2)), back_to_partner],
        [UNITS[:3], None],
    ]
    last_at = min(n for n, key in enumerate(rest) if key[0] < 2 and key[1][0] % NX in last_pair)
    for n, key in enumerate(rest):
        while todo and (n >= 4 + 8 * (3 - len(todo)) or n >= last_at):
            units, after = todo.pop(0)
            for r, c in units:
                part_unit(r, c, last_pair)
            if after is not None:
                after(last_pair)
        back(*key)

    own = part_ref.at[x, z]
    summed(2, (0, 0))
    go(own.at[7:11], pland2_ref, p2_send, p2_recv, other_core)
    returns = [(region, xof(1), 3, 0), (region, xof(2), 4, 1)]
    returns += [(partner, xof(core + e), e, 2 + e) for e in range(2)]
    returns += [(outer, xof(core + e), 5 + e, 4 + e) for e in range(2)]
    returns += [(outer, xof(-d), 7 + xof(-d), 6 + x) for d in range(NX)]

    def give(k):
        reg, xx, strip, slot = returns[k]
        go(own.at[strip], dland2_ref.at[slot], d2_send.at[k], d2_recv.at[k], target(reg, xx, z))

    def turn_back(grp):
        stacked = ss_ref[grp].reshape(TILE, TILE).T
        for zz in range(NZ):
            msend2_ref[grp, zz] = stacked[ROWS * zz : ROWS * (zz + 1)]
        for k in range(1, NZ):
            go(
                msend2_ref.at[grp, zof(k)], mrecv2_ref.at[grp, z], m2_send.at[grp, k - 1], m2_recv.at[grp, k - 1],
                target(region, x, zof(k)),
            )
        mrecv2_ref[grp, z] = msend2_ref[grp, z]

    for k in range(6, 10):
        give(k)
    ss_ref[...] = jnp.zeros_like(ss_ref)
    summed(1, (0, 0))
    summed(0, (0, 0))
    ss_ref[0, 0] = part_ref[x, z, 3]
    for e in range(2):
        ss_ref[0, 1 + e] = part_ref[x, z, e]
        ss_ref[0, 3 + e] = part_ref[x, z, 5 + e]
    turn_back(0)
    for k in range(6):
        give(k)
    landed(pland2_ref, p2_send, p2_recv, other_core)
    ss_ref[1, 0:4] = pland2_ref[...]
    turn_back(1)

    potential_ref[...] = jnp.zeros_like(potential_ref)
    potential_ref[:, row_tile(region, x)] = part_ref[x, z, 2]
    places = [(region, xof(-1)), (region, xof(-2))]
    places += [(partner, xof(core - 1 - e)) for e in range(2)]
    places += [(outer, xof(core - 1 - e)) for e in range(2)]
    places += [(beyond, xof(d)) for d in range(NX)]
    for k, (reg, tile) in enumerate(places):
        slot = k if k < 6 else 6 + xof(k - 6)
        landed(dland2_ref.at[slot], d2_send.at[k], d2_recv.at[k], target(*returns[k][:2], z))
        potential_ref[:, row_tile(reg, tile)] += dland2_ref[slot]
    for grp, cols in enumerate((own_cols, past_cols)):
        for k in range(1, NZ):
            landed(
                mrecv2_ref.at[grp, zof(-k)], m2_send.at[grp, k - 1], m2_recv.at[grp, k - 1],
                target(region, x, zof(k)),
            )
        parts = swap_groups([mrecv2_ref[grp, zz] for zz in range(NZ)])
        for e, c in enumerate(cols):
            potential_ref[:, c] += parts[e]

    for copy in sent:
        copy.wait_send()


def on_device(density_matrix, basis, union, weights, in_scale, in_shift, hidden_weight, hidden_bias, out_weight):
    vmem = pl.BlockSpec(memory_space=pltpu.VMEM)
    hbm = pl.BlockSpec(memory_space=pl.ANY)
    f32, bf16 = jnp.float32, jnp.bfloat16
    dma = pltpu.SemaphoreType.DMA
    count = len(CLASSES) * NN
    strip = (ROWS, TILE)
    width = in_scale.shape[0]
    row = pltpu.VMEM((1, width), f32)
    scratch = [
        pltpu.VMEM(density_matrix.shape, f32),
        pltpu.VMEM((2, PB, U * TILE), f32),
        pltpu.VMEM(weights.shape, f32),
        row, row, pltpu.VMEM((width, width), f32), row, row,
        pltpu.VMEM((NP, 3 * REG), f32),
        pltpu.VMEM((3, NP, 3 * REG), bf16),
        pltpu.VMEM((3 * REG, NP), bf16),
        pltpu.VMEM((3 * REG, NP), bf16),
        pltpu.VMEM((NP, 3 * REG), bf16),
        pltpu.VMEM((NP, 3 * REG), bf16),
        pltpu.VMEM((3 * REG, 2 * TILE), bf16),
        pltpu.VMEM((NP, TILE), f32),
        pltpu.VMEM((REG, 2 * TILE), f32),
        pltpu.VMEM((NX, NZ, STRIPS) + strip, f32),
        pltpu.VMEM((NX, NZ, SHARED) + strip, f32),
        pltpu.VMEM((NX, NZ, SHARED) + strip, f32),
        pltpu.VMEM((NX, NZ, STRIPS) + strip, f32),
        pltpu.VMEM((NX, NZ, SHARED) + strip, f32),
        pltpu.VMEM((NX, NZ, SHARED) + strip, f32),
        pltpu.VMEM((NN, STRIPS) + strip, f32),
        pltpu.VMEM((NX, NZ, SHARED) + strip, f32),
        pltpu.VMEM((NX, NZ, SHARED) + strip, f32),
        pltpu.VMEM((2, NZ) + strip, f32),
        pltpu.VMEM((2, NZ) + strip, f32),
        pltpu.VMEM((4,) + strip, f32),
        pltpu.VMEM((10,) + strip, f32),
        pltpu.VMEM((4,) + strip, f32),
        pltpu.VMEM((2, NZ) + strip, f32),
        pltpu.VMEM((2, NZ) + strip, f32),
        pltpu.VMEM((2, 8) + strip, f32),
        pltpu.VMEM((10,) + strip, f32),
        pltpu.VMEM((4,) + strip, f32),
        dma((8,)), dma((count,)), dma((count,)), dma((count,)), dma((count,)),
        dma((NX,)), dma((NX,)), dma((NX,)), dma((NX,)),
        dma((NX * NZ,)), dma((NX * NZ,)), dma((NX * NZ,)), dma((NX * NZ,)),
        dma((2, NZ - 1)), dma((2, NZ - 1)), dma((10,)), dma((10,)), dma, dma,
        dma((2, NZ - 1)), dma((2, NZ - 1)), dma((10,)), dma((10,)), dma, dma,
    ]
    density, potential = pl.pallas_call(
        kernel,
        out_shape=(
            jax.ShapeDtypeStruct(weights.shape, f32),
            jax.ShapeDtypeStruct(density_matrix.shape, f32),
        ),
        in_specs=[
            pl.BlockSpec(memory_space=pltpu.SMEM), hbm, hbm, hbm, hbm, hbm, hbm, hbm, hbm,
        ],
        out_specs=(vmem, vmem),
        scratch_shapes=scratch,
        compiler_params=pltpu.CompilerParams(
            collective_id=0, has_side_effects=True, vmem_limit_bytes=66_000_000
        ),
    )(
        union, density_matrix, basis, weights,
        in_scale[None], in_shift[None], hidden_weight, hidden_bias[None], out_weight[None],
    )
    return density, potential


def solution(mesh):
    own = P(("space", "dev"), None)
    in_specs = (own, P(("space", "dev"), None, None), own, own, P(), P(), P(), P(), P())
    return jax.shard_map(on_device, mesh=mesh, in_specs=in_specs, out_specs=(own, own), check_vma=False)
```
